128 devices in a mesh: ctx: 32 (over z, x, core), mp: 4 (over y).
Axes of the slice: x: 4, y: 4, z: 4, core: 2. Of those that a mesh axis runs over, the one named last changes fastest.
Arguments:
- query_one: bfloat16 [4096, 65536], P('mp', 'ctx'), may hold values from -6 to 6
- key_one: bfloat16 [4096, 65536], P('mp', 'ctx'), may hold values from -6 to 6
- value_one: bfloat16 [4096, 65536], P('mp', 'ctx'), may hold values from -6 to 6
- query_two: bfloat16 [4096, 65536], P('mp', 'ctx'), may hold values from -6 to 6
- key_two: bfloat16 [4096, 65536], P('mp', 'ctx'), may hold values from -6 to 6
- conv_weights: float32 [2, 3, 3, 4096], P(None, None, None, 'mp'), may hold values from -3 to 3
- mr_filter: bfloat16 [256, 128], P('mp'), may hold values from -0.5 to 0.5
- li_rate: float32 [256, 16], P('mp'), may hold values from 1.5258789e-07 to 0.08
- li_residue: float32 [256, 16], P('mp'), may hold values from -1.5 to 1.5
- norm_gain: float32 [4096], P('mp'), may hold values from 0.1 to 1.9
Outputs:
- normed: bfloat16 [4096, 65536], P('mp', 'ctx')
The draws below stay inside these ranges and needn't reach their ends.
All inputs are finite; a program needn't handle non-finite values.
Results may differ from the reference program's by a relative error of at most 0.0075.
Values may be sent and summed in bfloat16 or wider, within the bound.
A program may use at most 192 MiB of HBM per device.

```python
import math
import jax
import jax.numpy as jnp
from jax import lax

D = 4096
GROUP = 16
MR_LEN = 128
LI_BLOCK = 256
MODES = 16
SEQ = 65536
FILTERS = 256


def shard_levels(rng, shape, pieces, least, top_value):
    gain = 1.0
    for axis_at, shards_of in pieces:
        heights = jax.random.uniform(jax.random.fold_in(jax.random.fold_in(rng, 6), axis_at), (shards_of,), jnp.float32, least / len(pieces), top_value / len(pieces))
        gain = gain * jnp.repeat(jnp.exp(heights), shape[axis_at] // shards_of).reshape((-1,) + (1,) * (len(shape) - 1 - axis_at))
    return gain


def bell_draw(stream_key, extent, deviation, limit, split=(), held_as=jnp.bfloat16):
    values = deviation * jax.random.normal(stream_key, extent, jnp.float32)
    if split:
        values = values * shard_levels(stream_key, extent, split, -0.22, 0.18)
    return jnp.clip(values, -limit, limit).astype(held_as)


def setup_inputs(seed: int = 0) -> dict:
    key_list = jax.random.split(jax.random.key(seed), 11)
    query_one = bell_draw(key_list[0], (D, SEQ), 1.0, 6.0, ((0, 4), (1, 32)))
    key_one = bell_draw(key_list[1], (D, SEQ), 1.0, 6.0, ((0, 4), (1, 32)))
    value_one = bell_draw(key_list[2], (D, SEQ), 1.0, 6.0, ((0, 4), (1, 32)))
    query_two = bell_draw(key_list[3], (D, SEQ), 1.0, 6.0, ((0, 4), (1, 32)))
    key_two = bell_draw(key_list[4], (D, SEQ), 1.0, 6.0, ((0, 4), (1, 32)))
    conv_weights = bell_draw(key_list[5], (2, 3, 3, D), 0.6, 3.0, ((3, 4),), jnp.float32)
    mr_filter = bell_draw(key_list[6], (FILTERS, MR_LEN), MR_LEN ** -0.5, 0.5, ((0, 4),))
    li_rate = jnp.clip(jnp.exp(math.log(0.08) - 13.169796 * jax.random.uniform(key_list[7], (FILTERS, MODES), jnp.float32) ** shard_levels(key_list[7], (FILTERS, MODES), ((0, 4),), -0.2, 0.2)), 1.5258788721439487e-07, 0.08)
    li_residue = bell_draw(key_list[8], (FILTERS, MODES), 0.25, 1.5, ((0, 4),), jnp.float32)
    norm_gain = jnp.clip(1.0 + 0.18 * jax.random.normal(key_list[9], (D,), jnp.float32), 0.1, 1.9)
    return {"query_one": query_one, "key_one": key_one, "value_one": value_one, "query_two": query_two, "key_two": key_two, "conv_weights": conv_weights, "mr_filter": mr_filter, "li_rate": li_rate, "li_residue": li_residue, "norm_gain": norm_gain}


lane_width = 128

def short_filter(extended, weights):
    as_float = extended.astype(jnp.float32)
    return weights[0][:, None] * as_float[:, 2:] + weights[1][:, None] * as_float[:, 1:-1] + weights[2][:, None] * as_float[:, :-2]

def causal_short(values, weights):
    padding = jnp.zeros((values.shape[0], 2), values.dtype)
    return short_filter(jnp.concatenate([padding, values], axis=1), weights)

def medium_kernel(taps):
    group_count, tap_count = taps.shape
    pattern = jnp.concatenate([jnp.zeros((group_count, 1), taps.dtype), jnp.flip(taps, axis=1), jnp.zeros((group_count, 2 * tap_count - 1), taps.dtype)], axis=1)
    tiled = jnp.tile(pattern, (1, tap_count))[:, :tap_count * (3 * tap_count - 1)]
    skewed = tiled.reshape(group_count, tap_count, 3 * tap_count - 1)[:, :, :2 * tap_count]
    return jnp.swapaxes(skewed, 1, 2)

def filter_tables(rate, residue, block_size):
    lag_values = jnp.arange(block_size, dtype=jnp.float32)
    amplitude = residue * jnp.sqrt(rate)
    decay = jnp.exp(-rate[:, :, None] * lag_values)
    difference = jnp.arange(block_size, dtype=jnp.int32)[None, :] - jnp.arange(block_size, dtype=jnp.int32)[:, None]
    lag_grid = jnp.clip(difference, 0, block_size - 1).astype(jnp.float32)
    toeplitz = jnp.zeros((rate.shape[0], block_size, block_size), jnp.float32)
    for mode_index in range(rate.shape[1]):
        toeplitz = toeplitz + amplitude[:, mode_index, None, None] * jnp.exp(-rate[:, mode_index, None, None] * lag_grid[None])
    kernel_block = jnp.where((difference >= 0)[None], toeplitz, jnp.zeros_like(toeplitz)).astype(jnp.bfloat16)
    input_projection = jnp.flip(decay, axis=2).astype(jnp.bfloat16)
    output_readout = amplitude[:, :, None] * decay * jnp.exp(-rate)[:, :, None]
    stride_decay = jnp.exp(-rate * block_size)
    return (kernel_block, input_projection, output_readout, stride_decay)

def medium_filter(extended, kernel, group_width):
    tap_count = kernel.shape[2]
    chan_count = extended.shape[0]
    out_rows = extended.shape[1] - tap_count
    count_of_groups = chan_count // group_width
    count_of_blocks = out_rows // tap_count
    first_half = extended[:, :out_rows].reshape(count_of_groups, group_width * count_of_blocks, tap_count).astype(jnp.float32)
    second_half = extended[:, tap_count:].reshape(count_of_groups, group_width * count_of_blocks, tap_count).astype(jnp.float32)
    kernel_float = kernel.astype(jnp.float32)
    mixed = jnp.einsum('gmk,gki->gmi', first_half, kernel_float[:, :tap_count], precision=lax.Precision.HIGHEST)
    mixed = mixed + jnp.einsum('gmk,gki->gmi', second_half, kernel_float[:, tap_count:], precision=lax.Precision.HIGHEST)
    return mixed.reshape(chan_count, out_rows)

def chain_pair(earlier, later):
    return (earlier[0] * later[0], later[0] * earlier[1] + later[1])

def long_filter(values, tables, start_state):
    kernel_block, input_projection, output_readout, stride_decay = tables
    count_of_groups, group_width, row_count = values.shape
    block_size = kernel_block.shape[1]
    count_of_blocks = row_count // block_size
    count_of_modes = input_projection.shape[1]
    sequence_pieces = values.reshape(count_of_groups, group_width * count_of_blocks, block_size).astype(jnp.float32)
    within = jnp.einsum('gmj,gji->gmi', sequence_pieces, kernel_block.astype(jnp.float32), precision=lax.Precision.HIGHEST)
    local_partial_terms = jnp.einsum('phw,psw->phs', sequence_pieces, input_projection.astype(jnp.float32), precision=lax.Precision.HIGHEST)
    local_partial_terms = local_partial_terms.reshape(count_of_groups, group_width, count_of_blocks, count_of_modes)
    decay_four = stride_decay[:, None, None, :]
    local_partial_terms = jnp.concatenate([local_partial_terms[:, :, :1] + decay_four * start_state[:, :, None], local_partial_terms[:, :, 1:]], axis=2)
    factor = jnp.broadcast_to(decay_four, local_partial_terms.shape)
    _, states = lax.associative_scan(chain_pair, (factor, local_partial_terms), axis=2)
    preceding_rows = jnp.concatenate([start_state[:, :, None], states[:, :, :-1]], axis=2)
    carried_state = jnp.einsum('dkp,dps->dks', preceding_rows.reshape(count_of_groups, group_width * count_of_blocks, count_of_modes), output_readout, precision=lax.Precision.HIGHEST)
    return ((within + carried_state).reshape(count_of_groups, group_width, row_count), states[:, :, -1])

def reference(query_one, key_one, value_one, query_two, key_two, conv_weights, mr_filter, li_rate, li_residue, norm_gain):
    chan_total, seq_rows = query_one.shape
    block_total = chan_total // lane_width
    per_block = lane_width // GROUP

    def split_channels(array):
        return array.reshape(block_total, lane_width, seq_rows)
    weight_blocks = jnp.moveaxis(conv_weights.reshape(2, 3, 3, block_total, lane_width), 3, 0)
    filter_blocks = mr_filter.reshape(block_total, per_block, MR_LEN)
    rate_blocks = li_rate.reshape(block_total, per_block, MODES)
    residue_blocks = li_residue.reshape(block_total, per_block, MODES)

    def one_block(item):
        query_a, key_a, value_a, query_b, key_b, weights, taps, rate, residue = item
        query_conv = causal_short(query_a, weights[0, 0])
        key_conv = causal_short(key_a, weights[0, 1])
        value_conv = causal_short(value_a, weights[0, 2])
        product = (key_conv * value_conv).astype(jnp.bfloat16)
        extended = jnp.concatenate([jnp.zeros((lane_width, MR_LEN), jnp.bfloat16), product], axis=1)
        mixed = medium_filter(extended, medium_kernel(taps), GROUP)
        layer_one = (query_conv * mixed).astype(jnp.bfloat16)
        query_next = causal_short(query_b, weights[1, 0])
        key_next = causal_short(key_b, weights[1, 1])
        value_next = causal_short(layer_one, weights[1, 2])
        second = (key_next * value_next).astype(jnp.bfloat16)
        tables = filter_tables(rate, residue, LI_BLOCK)
        start_state = jnp.zeros((per_block, GROUP, MODES), jnp.float32)
        result, _ = long_filter(second.reshape(per_block, GROUP, seq_rows), tables, start_state)
        result = result.reshape(lane_width, seq_rows).astype(jnp.bfloat16)
        return query_next * result.astype(jnp.float32)
    gated = lax.map(one_block, (split_channels(query_one), split_channels(key_one), split_channels(value_one), split_channels(query_two), split_channels(key_two), weight_blocks, filter_blocks, rate_blocks, residue_blocks))
    gated = gated.reshape(chan_total, seq_rows)
    total = lax.optimization_barrier(jnp.sum(gated * gated, axis=0, keepdims=True))
    return (gated * lax.rsqrt(total / chan_total + 1e-05) * norm_gain[:, None]).astype(jnp.bfloat16)
```

```python
import functools

import jax
import jax.numpy as jnp
from jax import lax
from jax.experimental import pallas as pl
from jax.experimental.pallas import tpu as pltpu
from jax.sharding import PartitionSpec as P

GROUP = 16
TAPS = 128
BLOCK = 256
MODES = 16
LANES = 128
MESH = pl.DeviceIdType.MESH
F32 = jnp.float32
BF16 = jnp.bfloat16
Q1, K1, V1, K2, Q2 = range(5)


def aligned(index, size):
    return pl.ds(pl.multiple_of(index * size, size), size)


def lane_ids(rows, cols):
    return lax.broadcasted_iota(jnp.int32, (rows, cols), 1)


def split_pair(x):
    high = x.astype(BF16)
    low = (x - high.astype(F32)).astype(BF16)
    return high, low


def short_filter(x, taps):
    w0, w1, w2 = taps
    return w0 * x + w1 * pltpu.roll(x, 1, 1) + w2 * pltpu.roll(x, 2, 1)


def to_rows(x, first, count, step, width):
    return jnp.concatenate(
        [x[:, first + i * step : first + i * step + width] for i in range(count)], axis=0
    )


def kernel(
    n_ctx, n_mp, q1, k1, v1, k2, q2, cw, mr, rate, residue, gain, out,
    xin, hwide, hthin, wmed, wlong, readout, proj, ptwo, within, qnext, state, wcol,
    pad, tapf, rate_t, res_t, fin, decay, got, carry, back, sums, sums_in,
    in_sem, hsend, hrecv, asend, arecv, bsend, brecv, msend, mrecv, osem,
):
    me = lax.axis_index("ctx")
    my_mp = lax.axis_index("mp")
    right = lax.rem(me + 1, n_ctx)
    chans, length = xin.shape[1:]
    tiles = chans // LANES
    per_tile = LANES // GROUP
    groups = chans // GROUP
    blocks = length // BLOCK
    med_blocks = length // TAPS
    share = tiles * MODES // n_ctx
    cuts = MODES // share
    streams = (q1, k1, v1, k2, q2)

    def load_copy(s, t):
        rows = aligned(t, LANES)
        return pltpu.make_async_copy(streams[s].at[rows, :], xin.at[s, rows, :], in_sem.at[s, t])

    def halo_copy(s, t):
        rows = aligned(t, LANES)
        wide = s in (K1, V1)
        width = 2 * LANES if wide else LANES
        target = hwide.at[s - K1, rows, :] if wide else hthin.at[{Q1: 0, K2: 1, Q2: 2}[s], rows, :]
        return pltpu.make_async_remote_copy(
            src_ref=streams[s].at[rows, pl.ds(length - width, width)],
            dst_ref=target,
            send_sem=hsend.at[s, t],
            recv_sem=hrecv.at[s, t],
            device_id={"ctx": right},
            device_id_type=MESH,
        )

    first_four = (K1, V1, Q1, K2)

    def start_loads(t, _):
        for s in first_four:
            load_copy(s, t).start()
        return _

    lax.fori_loop(0, tiles, start_loads, 0)

    def start_late(t, _):
        load_copy(Q2, t).start()
        return _

    lax.fori_loop(0, tiles, start_late, 0)

    barrier = pltpu.get_barrier_semaphore()

    def greet_ctx(i, _):
        pl.semaphore_signal(
            barrier, inc=1, device_id={"ctx": lax.rem(me + i, n_ctx)}, device_id_type=MESH
        )
        return _

    lax.fori_loop(1, n_ctx, greet_ctx, 0)
    for i in range(1, n_mp):
        pl.semaphore_signal(
            barrier, inc=1, device_id={"mp": lax.rem(my_mp + i, n_mp)}, device_id_type=MESH
        )

    pad[...] = jnp.zeros_like(pad)
    for layer in range(2):
        for stream in range(3):
            for tap in range(3):
                at = layer * 9 + stream * 3 + tap
                pad[at : at + 1, :] = cw[layer, stream, tap : tap + 1, :]
    pad[18:19, :] = gain[...]
    for t in range(tiles):
        wcol[t * LANES : (t + 1) * LANES, :] = pad[:, t * LANES : (t + 1) * LANES].T
    tapf[...] = mr[...].astype(F32)
    pad[...] = jnp.zeros_like(pad)
    pad[0:groups, 0:MODES] = rate[...]
    rate_t[...] = pad[:, 0:LANES].T[0:MODES, :]
    pad[0:groups, 0:MODES] = residue[...]
    res_t[...] = pad[:, 0:LANES].T[0:MODES, :]

    def mode_column(table, g):
        hit = lane_ids(MODES, LANES) == g
        return jnp.sum(jnp.where(hit, table[...], 0.0), axis=1, keepdims=True)

    def circulant(row):
        return pltpu.roll(
            jnp.broadcast_to(row, (LANES, LANES)), 0, 1, stride=1, stride_axis=0
        )

    def tables(g, _):
        above = lane_ids(LANES, LANES) >= lax.broadcasted_iota(jnp.int32, (LANES, LANES), 0)
        rate_c = mode_column(rate_t, g)
        amp = mode_column(res_t, g) * jnp.sqrt(rate_c)
        lag = lane_ids(1, BLOCK).astype(F32)
        fall = jnp.exp(-rate_c * lag)
        proj[g] = jnp.exp(-rate_c * (float(BLOCK - 1) - lag)).astype(BF16)
        tall = amp * fall
        high, low = split_pair(tall * jnp.exp(-rate_c))
        readout[g] = jnp.concatenate([high, low, high], axis=0)
        taps_h = jnp.sum(tall, axis=0, keepdims=True)
        near = circulant(taps_h[:, :LANES])
        far = circulant(taps_h[:, LANES:])
        diagonal = jnp.where(above, near, 0.0).astype(BF16)
        wlong[g, 0:LANES, 0:LANES] = diagonal
        wlong[g, LANES:, LANES:] = diagonal
        wlong[g, 0:LANES, LANES:] = jnp.where(above, far, near).astype(BF16)
        wlong[g, LANES:, 0:LANES] = jnp.zeros((LANES, LANES), BF16)
        short = circulant(tapf[pl.ds(g, 1), :])
        wmed[g, 0:LANES, :] = jnp.where(above, 0.0, short).astype(BF16)
        wmed[g, LANES:, :] = jnp.where(above, short, 0.0).astype(BF16)
        return _

    early = groups // 2
    lax.fori_loop(0, early, tables, 0)
    pl.semaphore_wait(barrier, n_ctx - 1 + n_mp - 1)

    def start_halos(t, _):
        for s in first_four:
            halo_copy(s, t).start()
        return _

    lax.fori_loop(0, tiles, start_halos, 0)

    def start_late_halos(t, _):
        halo_copy(Q2, t).start()
        return _

    lax.fori_loop(0, tiles, start_late_halos, 0)
    lax.fori_loop(early, groups, tables, 0)

    keep = me > 0

    def columns(rows, layer, stream):
        at = layer * 9 + stream * 3
        return [wcol[rows, at + tap : at + tap + 1] for tap in range(3)]

    def extended(s, rows):
        wide = s in (K1, V1)
        halo = hwide[s - K1, rows, :] if wide else hthin[{Q1: 0, K2: 1, Q2: 2}[s], rows, :]
        halo = jnp.where(keep, halo.astype(F32), 0.0)
        return jnp.concatenate([halo, xin[s, rows, :].astype(F32)], axis=1)

    def produce(g, t, i):
        rows = aligned(g, GROUP)
        key = short_filter(extended(K1, rows), columns(rows, 0, 1))
        value = short_filter(extended(V1, rows), columns(rows, 0, 2))
        product = (key * value).astype(BF16)
        mixed = jnp.dot(
            to_rows(product, 0, med_blocks + 1, TAPS, 2 * TAPS), wmed[g], preferred_element_type=F32
        )
        mixed = jnp.concatenate(
            [mixed[j * GROUP : (j + 1) * GROUP, :] for j in range(med_blocks + 1)], axis=1
        )
        query = short_filter(extended(Q1, rows), columns(rows, 0, 0))
        layer_one = (query * mixed).astype(BF16).astype(F32)
        value_two = short_filter(layer_one, columns(rows, 1, 2))[:, LANES:]
        key_two = short_filter(extended(K2, rows), columns(rows, 1, 1))[:, LANES:]
        second = (key_two * value_two).astype(BF16)
        pieces = to_rows(second, 0, blocks, BLOCK, BLOCK)
        ptwo[g] = pieces
        local = lax.dot_general(
            proj[g], pieces, (((1,), (1,)), ((), ())), preferred_element_type=F32
        )
        rate_c = mode_column(rate_t, g)
        lane = lane_ids(MODES, GROUP * blocks)
        total = local
        width = 1
        while width < blocks:
            moved = pltpu.roll(total, width * GROUP, 1)
            factor = jnp.exp(-rate_c * float(BLOCK * width))
            total = total + jnp.where(lane >= width * GROUP, factor * moved, 0.0)
            width *= 2
        state[g] = jnp.where(lane >= GROUP, pltpu.roll(total, GROUP, 1), 0.0)
        spot = lax.shift_right_logical(lane, 4) == i
        moved = pltpu.roll(total, lax.rem(i * GROUP + GROUP, LANES), 1)
        drop = jnp.exp(-rate_c * float(length))
        for c in range(cuts):
            part = slice(c * share, (c + 1) * share)
            at = t * cuts + c
            fin[at] = jnp.where(spot[part], moved[part], fin[at])
            decay[at] = jnp.where(spot[part], jnp.broadcast_to(drop, moved.shape)[part], decay[at])

    fin[...] = jnp.zeros_like(fin)
    decay[...] = jnp.zeros_like(decay)

    def tile_step(t, _):
        for s in first_four:
            load_copy(s, t).wait()
            halo_copy(s, t).wait_recv()

        def group_step(i, _):
            produce(t * per_tile + i, t, i)
            return _

        return lax.fori_loop(0, per_tile, group_step, _)

    lax.fori_loop(0, tiles, tile_step, 0)

    def state_copy(peer):
        return pltpu.make_async_remote_copy(
            src_ref=fin.at[peer],
            dst_ref=got.at[me],
            send_sem=asend.at[peer],
            recv_sem=arecv.at[me],
            device_id={"ctx": peer},
            device_id_type=MESH,
        )

    def state_arrival(peer):
        return pltpu.make_async_remote_copy(
            src_ref=fin.at[peer],
            dst_ref=got.at[peer],
            send_sem=asend.at[peer],
            recv_sem=arecv.at[peer],
            device_id={"ctx": peer},
            device_id_type=MESH,
        )

    def carry_copy(peer):
        return pltpu.make_async_remote_copy(
            src_ref=carry.at[peer],
            dst_ref=back.at[me],
            send_sem=bsend.at[peer],
            recv_sem=brecv.at[me],
            device_id={"ctx": peer},
            device_id_type=MESH,
        )

    def carry_arrival(peer):
        return pltpu.make_async_remote_copy(
            src_ref=carry.at[peer],
            dst_ref=back.at[peer],
            send_sem=bsend.at[peer],
            recv_sem=brecv.at[peer],
            device_id={"ctx": peer},
            device_id_type=MESH,
        )

    def each_peer(act):
        def step(i, _):
            act(lax.rem(me + i, n_ctx))
            return _

        lax.fori_loop(1, n_ctx, step, 0)

    each_peer(lambda peer: state_copy(peer).start())
    got[me] = fin[me]

    def inner_part(t, _):
        load_copy(Q2, t).wait()
        halo_copy(Q2, t).wait_recv()

        def group_step(i, _):
            g = t * per_tile + i
            rows = aligned(g, GROUP)
            within[g] = jnp.dot(ptwo[g], wlong[g], preferred_element_type=F32)
            query = short_filter(extended(Q2, rows), columns(rows, 1, 0))[:, LANES:]
            qnext[g] = to_rows(query, 0, blocks, BLOCK, BLOCK)
            return _

        return lax.fori_loop(0, per_tile, group_step, _)

    half = (tiles + 1) // 2
    lax.fori_loop(0, half, inner_part, 0)
    each_peer(lambda peer: state_arrival(peer).wait_recv())

    def chain(d, value):
        carry[d] = value
        return value * decay[me] + got[d]

    lax.fori_loop(0, n_ctx, chain, jnp.zeros((share, LANES), F32))
    each_peer(lambda peer: carry_copy(peer).start())
    back[me] = carry[me]
    lax.fori_loop(half, tiles, inner_part, 0)
    each_peer(lambda peer: carry_arrival(peer).wait_recv())

    sums[...] = jnp.zeros_like(sums)

    def finish_tile(t, _):
        incoming = jnp.concatenate([back[t * cuts + c] for c in range(cuts)], axis=0)

        def group_step(i, _):
            g = t * per_tile + i
            lane = lane_ids(MODES, LANES)
            seed = jnp.where(
                lane < GROUP, pltpu.roll(incoming, lax.rem(LANES - i * GROUP, LANES), 1), 0.0
            )
            width = 1
            while width < blocks:
                seed = seed + pltpu.roll(seed, width * GROUP, 1)
                width *= 2
            rate_c = mode_column(rate_t, g)
            block_at = lax.shift_right_logical(lane, 4).astype(F32)
            total = state[g] + seed * jnp.exp(-rate_c * (block_at * float(BLOCK)))
            high, low = split_pair(total)
            stacked = jnp.concatenate([high, high, low], axis=0)
            carried = lax.dot_general(
                stacked, readout[g], (((0,), (0,)), ((), ())), preferred_element_type=F32
            )
            long_two = (within[g] + carried).astype(BF16).astype(F32)
            gated = qnext[g] * long_two
            within[g] = gated
            square = gated * gated
            for b in range(blocks):
                low_rows = square[b * GROUP : b * GROUP + 8, :]
                sums[b] = sums[b] + (low_rows + square[b * GROUP + 8 : (b + 1) * GROUP, :])
            return _

        return lax.fori_loop(0, per_tile, group_step, _)

    lax.fori_loop(0, tiles, finish_tile, 0)

    sums_in[my_mp] = jnp.sum(sums[...], axis=1)

    def sum_copy(peer, place):
        return pltpu.make_async_remote_copy(
            src_ref=sums_in.at[my_mp],
            dst_ref=sums_in.at[place],
            send_sem=msend.at[peer],
            recv_sem=mrecv.at[place],
            device_id={"mp": peer},
            device_id_type=MESH,
        )

    mp_peers = [lax.rem(my_mp + i, n_mp) for i in range(1, n_mp)]
    for peer in mp_peers:
        sum_copy(peer, my_mp).start()
    for peer in mp_peers:
        sum_copy(peer, peer).wait_recv()
    whole = sums_in[0]
    for i in range(1, n_mp):
        whole = whole + sums_in[i]
    scale = lax.rsqrt(whole / float(n_mp * chans) + 1e-05)
    sums[...] = jnp.broadcast_to(scale[:, None, :], sums.shape)

    def out_copy(t):
        rows = aligned(t, LANES)
        return pltpu.make_async_copy(xin.at[Q1, rows, :], out.at[rows, :], osem.at[t])

    def scale_tile(t, _):
        def group_step(i, _):
            g = t * per_tile + i
            rows = aligned(g, GROUP)
            gain_c = wcol[rows, 18:19]
            gated = within[g]
            for b in range(blocks):
                scale_b = jnp.concatenate([sums[b], sums[b]], axis=0)
                piece = gated[b * GROUP : (b + 1) * GROUP, :] * scale_b * gain_c
                xin[Q1, rows, b * BLOCK : (b + 1) * BLOCK] = piece.astype(BF16)
            return _

        lax.fori_loop(0, per_tile, group_step, 0)
        out_copy(t).start()
        return _

    lax.fori_loop(0, tiles, scale_tile, 0)

    for peer in mp_peers:
        sum_copy(peer, my_mp).wait_send()
    each_peer(lambda peer: state_copy(peer).wait_send())
    each_peer(lambda peer: carry_copy(peer).wait_send())

    def drain(t, _):
        for s in range(5):
            halo_copy(s, t).wait_send()
        out_copy(t).wait()
        return _

    lax.fori_loop(0, tiles, drain, 0)


def per_device(n_ctx, n_mp, query_one, key_one, value_one, query_two, key_two, conv_weights,
               mr_filter, li_rate, li_residue, norm_gain):
    chans, length = query_one.shape
    groups = chans // GROUP
    tiles = chans // LANES
    blocks = length // BLOCK
    share = tiles * MODES // n_ctx
    any_spec = pl.BlockSpec(memory_space=pl.ANY)
    vmem_spec = pl.BlockSpec(memory_space=pltpu.VMEM)
    dma = pltpu.SemaphoreType.DMA
    message = pltpu.VMEM((n_ctx, share, LANES), F32)
    return pl.pallas_call(
        functools.partial(kernel, n_ctx, n_mp),
        out_shape=jax.ShapeDtypeStruct((chans, length), BF16),
        in_specs=[any_spec] * 5 + [vmem_spec] * 5,
        out_specs=any_spec,
        scratch_shapes=[
            pltpu.VMEM((5, chans, length), BF16),
            pltpu.VMEM((2, chans, 2 * LANES), BF16),
            pltpu.VMEM((3, chans, LANES), BF16),
            pltpu.VMEM((groups, 2 * TAPS, TAPS), BF16),
            pltpu.VMEM((groups, BLOCK, BLOCK), BF16),
            pltpu.VMEM((groups, 3 * MODES, BLOCK), BF16),
            pltpu.VMEM((groups, MODES, BLOCK), BF16),
            pltpu.VMEM((groups, GROUP * blocks, BLOCK), BF16),
            pltpu.VMEM((groups, GROUP * blocks, BLOCK), F32),
            pltpu.VMEM((groups, GROUP * blocks, BLOCK), F32),
            pltpu.VMEM((groups, MODES, LANES), F32),
            pltpu.VMEM((chans, LANES), F32),
            pltpu.VMEM((LANES, chans), F32),
            pltpu.VMEM((groups, TAPS), F32),
            pltpu.VMEM((MODES, LANES), F32),
            pltpu.VMEM((MODES, LANES), F32),
            message,
            message,
            message,
            message,
            message,
            pltpu.VMEM((blocks, 8, BLOCK), F32),
            pltpu.VMEM((n_mp, blocks, BLOCK), F32),
            dma((5, tiles)),
            dma((5, tiles)),
            dma((5, tiles)),
            dma((n_ctx,)),
            dma((n_ctx,)),
            dma((n_ctx,)),
            dma((n_ctx,)),
            dma((n_mp,)),
            dma((n_mp,)),
            dma((tiles,)),
        ],
        compiler_params=pltpu.CompilerParams(
            collective_id=0, has_side_effects=True, vmem_limit_bytes=67043328
        ),
        name="hyena_pair",
    )(
        query_one, key_one, value_one, key_two, query_two,
        conv_weights, mr_filter, li_rate, li_residue, norm_gain.reshape(1, chans),
    )


def solution(mesh):
    in_specs = (
        P("mp", "ctx"),
        P("mp", "ctx"),
        P("mp", "ctx"),
        P("mp", "ctx"),
        P("mp", "ctx"),
        P(None, None, None, "mp"),
        P("mp", None),
        P("mp", None),
        P("mp", None),
        P("mp"),
    )
    return jax.shard_map(
        functools.partial(per_device, mesh.shape["ctx"], mesh.shape["mp"]),
        mesh=mesh,
        in_specs=in_specs,
        out_specs=P("mp", "ctx"),
        check_vma=False,
    )
```

```python
import functools

import jax
import jax.numpy as jnp
from jax import lax
from jax.experimental import pallas as pl
from jax.experimental.pallas import tpu as pltpu
from jax.sharding import PartitionSpec as P

GROUP = 16
TAPS = 128
BLOCK = 256
MODES = 16
LANES = 128
MESH = pl.DeviceIdType.MESH
F32 = jnp.float32
BF16 = jnp.bfloat16
Q1, K1, V1, K2, Q2 = range(5)


def aligned(index, size):
    return pl.ds(pl.multiple_of(index * size, size), size)


def lane_ids(rows, cols):
    return lax.broadcasted_iota(jnp.int32, (rows, cols), 1)


def split_pair(x):
    high = x.astype(BF16)
    low = (x - high.astype(F32)).astype(BF16)
    return high, low


def short_filter(x, taps):
    w0, w1, w2 = taps
    back_one = pltpu.roll(x, 1, 1).astype(F32)
    back_two = pltpu.roll(x, 2, 1).astype(F32)
    return w0 * x.astype(F32) + w1 * back_one + w2 * back_two


def grouped(start, stop, size, act):
    def step(j, _):
        for i in range(size):
            act(start + j * size + i)
        return _

    lax.fori_loop(0, (stop - start) // size, step, 0)


def to_rows(x, first, count, step, width):
    return jnp.concatenate(
        [x[:, first + i * step : first + i * step + width] for i in range(count)], axis=0
    )


def kernel(
    n_ctx, n_mp, q1, k1, v1, k2, q2, cw, mr, rate, residue, gain, out,
    xin, hwide, hthin, wmed, wlong, readout, proj, ptwo, within, qnext, state, wcol,
    pad, tapf, rate_t, res_t, fade, prod, mid, carried_in, fin, decay, got, carry, back, sums, sums_in,
    in_sem, hsend, hrecv, asend, arecv, bsend, brecv, msend, mrecv, osem,
):
    me = lax.axis_index("ctx")
    my_mp = lax.axis_index("mp")
    right = lax.rem(me + 1, n_ctx)
    chans, length = xin.shape[1:]
    tiles = chans // LANES
    per_tile = LANES // GROUP
    groups = chans // GROUP
    blocks = length // BLOCK
    med_blocks = length // TAPS
    share = tiles * MODES // n_ctx
    cuts = MODES // share
    streams = (q1, k1, v1, k2, q2)

    def load_copy(s, t):
        rows = aligned(t, LANES)
        return pltpu.make_async_copy(streams[s].at[rows, :], xin.at[s, rows, :], in_sem.at[s, t])

    def halo_copy(s, t):
        rows = aligned(t, LANES)
        wide = s in (K1, V1)
        width = 2 * LANES if wide else LANES
        target = hwide.at[s - K1, rows, :] if wide else hthin.at[{Q1: 0, K2: 1, Q2: 2}[s], rows, :]
        return pltpu.make_async_remote_copy(
            src_ref=streams[s].at[rows, pl.ds(length - width, width)],
            dst_ref=target,
            send_sem=hsend.at[s, t],
            recv_sem=hrecv.at[s, t],
            device_id={"ctx": right},
            device_id_type=MESH,
        )

    first_four = (K1, V1, Q1, K2)

    def start_loads(t, _):
        for s in first_four:
            load_copy(s, t).start()
        return _

    lax.fori_loop(0, tiles, start_loads, 0)

    def start_late(t, _):
        load_copy(Q2, t).start()
        return _

    lax.fori_loop(0, tiles, start_late, 0)

    barrier = pltpu.get_barrier_semaphore()

    def greet_ctx(i, _):
        pl.semaphore_signal(
            barrier, inc=1, device_id={"ctx": lax.rem(me + i, n_ctx)}, device_id_type=MESH
        )
        return _

    lax.fori_loop(1, n_ctx, greet_ctx, 0)
    for i in range(1, n_mp):
        pl.semaphore_signal(
            barrier, inc=1, device_id={"mp": lax.rem(my_mp + i, n_mp)}, device_id_type=MESH
        )

    pad[...] = jnp.zeros_like(pad)
    for layer in range(2):
        for stream in range(3):
            for tap in range(3):
                at = layer * 9 + stream * 3 + tap
                pad[at : at + 1, :] = cw[stream, tap, layer : layer + 1, :]
    pad[18:19, :] = gain[...]
    for t in range(tiles):
        wcol[t * LANES : (t + 1) * LANES, :] = pad[:, t * LANES : (t + 1) * LANES].T
    tapf[...] = mr[...].astype(F32)
    rate_t[...] = jnp.zeros_like(rate_t)
    res_t[...] = jnp.zeros_like(res_t)
    rate_t[:, 0:groups] = rate[...]
    res_t[:, 0:groups] = residue[...]

    def mode_column(table, g):
        hit = lane_ids(MODES, LANES) == g
        return jnp.sum(jnp.where(hit, table[...], 0.0), axis=1, keepdims=True)

    def circulant(row):
        return pltpu.roll(
            jnp.broadcast_to(row, (LANES, LANES)), 0, 1, stride=1, stride_axis=0
        )

    def tables(g):
        above = lane_ids(LANES, LANES) >= lax.broadcasted_iota(jnp.int32, (LANES, LANES), 0)
        rate_c = mode_column(rate_t, g)
        amp = mode_column(res_t, g) * jnp.sqrt(rate_c)
        lag = lane_ids(1, BLOCK).astype(F32)
        fall = jnp.exp(-rate_c * lag)
        proj[g] = jnp.exp(-rate_c * (float(BLOCK - 1) - lag)).astype(BF16)
        tall = amp * fall
        high, low = split_pair(tall * jnp.exp(-rate_c))
        readout[g] = jnp.concatenate([high, low, high], axis=0)
        taps_h = jnp.sum(tall, axis=0, keepdims=True)
        near = circulant(taps_h[:, :LANES])
        far = circulant(taps_h[:, LANES:])
        diagonal = jnp.where(above, near, 0.0).astype(BF16)
        wlong[g, 0:LANES, 0:LANES] = diagonal
        wlong[g, LANES:, LANES:] = diagonal
        wlong[g, 0:LANES, LANES:] = jnp.where(above, far, near).astype(BF16)
        wlong[g, LANES:, 0:LANES] = jnp.zeros((LANES, LANES), BF16)
        short = circulant(tapf[pl.ds(g, 1), :])
        wmed[g, 0:LANES, :] = jnp.where(above, 0.0, short).astype(BF16)
        wmed[g, LANES:, :] = jnp.where(above, short, 0.0).astype(BF16)
        block_at = lax.shift_right_logical(lane_ids(MODES, LANES), 4).astype(F32)
        fade[g] = jnp.exp(-rate_c * (block_at * float(BLOCK)))

    early = groups // 2
    grouped(0, early, 4, tables)
    pl.semaphore_wait(barrier, n_ctx - 1 + n_mp - 1)

    def start_halos(t, _):
        for s in first_four:
            halo_copy(s, t).start()
        return _

    lax.fori_loop(0, tiles, start_halos, 0)

    def start_late_halos(t, _):
        halo_copy(Q2, t).start()
        return _

    lax.fori_loop(0, tiles, start_late_halos, 0)
    grouped(early, groups, 4, tables)

    def columns(rows, layer, stream):
        at = layer * 9 + stream * 3
        return [wcol[rows, at + tap : at + tap + 1] for tap in range(3)]

    def extended(s, rows):
        wide = s in (K1, V1)
        halo = hwide[s - K1, rows, :] if wide else hthin[{Q1: 0, K2: 1, Q2: 2}[s], rows, :]
        return jnp.concatenate([halo, xin[s, rows, :]], axis=1)

    def make_product(t, i):
        rows = aligned(t * per_tile + i, GROUP)
        key = short_filter(extended(K1, rows), columns(rows, 0, 1))
        value = short_filter(extended(V1, rows), columns(rows, 0, 2))
        prod[i] = (key * value).astype(BF16)

    def make_layer(t, i):
        g = t * per_tile + i
        rows = aligned(g, GROUP)
        mixed = jnp.dot(
            to_rows(prod[i], 0, med_blocks + 1, TAPS, 2 * TAPS), wmed[g], preferred_element_type=F32
        )
        mixed = jnp.concatenate(
            [mixed[j * GROUP : (j + 1) * GROUP, :] for j in range(med_blocks + 1)], axis=1
        )
        query = short_filter(extended(Q1, rows), columns(rows, 0, 0))
        mid[i] = (query * mixed).astype(BF16)

    def make_second(t, i):
        g = t * per_tile + i
        rows = aligned(g, GROUP)
        value_two = short_filter(mid[i], columns(rows, 1, 2))[:, LANES:]
        key_two = short_filter(extended(K2, rows), columns(rows, 1, 1))[:, LANES:]
        second = (key_two * value_two).astype(BF16)
        ptwo[g] = to_rows(second, 0, blocks, BLOCK, BLOCK)

    def make_states(t):
        lane = lane_ids(MODES, GROUP * blocks)
        ends = jnp.zeros((MODES, LANES), F32)
        drops = jnp.zeros((MODES, LANES), F32)
        for i in range(per_tile):
            g = t * per_tile + i
            total = lax.dot_general(
                proj[g], ptwo[g], (((1,), (1,)), ((), ())), preferred_element_type=F32
            )
            rate_c = mode_column(rate_t, g)
            width = 1
            while width < blocks:
                moved = pltpu.roll(total, width * GROUP, 1)
                factor = jnp.exp(-rate_c * float(BLOCK * width))
                total = total + jnp.where(lane >= width * GROUP, factor * moved, 0.0)
                width *= 2
            state[g] = jnp.where(lane >= GROUP, pltpu.roll(total, GROUP, 1), 0.0)
            spot = lax.shift_right_logical(lane, 4) == i
            moved = pltpu.roll(total, (i + 1) * GROUP % LANES, 1) if i + 1 < blocks else total
            ends = jnp.where(spot, moved, ends)
            drops = jnp.where(spot, jnp.exp(-rate_c * float(length)), drops)
        for c in range(cuts):
            part = slice(c * share, (c + 1) * share)
            fin[t * cuts + c] = ends[part]
            decay[t * cuts + c] = drops[part]

    def tile_step(t, _):
        for s in first_four:
            load_copy(s, t).wait()
            halo_copy(s, t).wait_recv()

        @pl.when(me == 0)
        def clear():
            rows = aligned(t, LANES)
            hwide[:, rows, :] = jnp.zeros((2, LANES, 2 * LANES), BF16)
            hthin[0:2, rows, :] = jnp.zeros((2, LANES, LANES), BF16)

        grouped(0, per_tile, 1, functools.partial(make_product, t))
        grouped(0, per_tile, 2, functools.partial(make_layer, t))
        grouped(0, per_tile, 1, functools.partial(make_second, t))
        make_states(t)
        return _

    lax.fori_loop(0, tiles, tile_step, 0)

    def state_copy(peer):
        return pltpu.make_async_remote_copy(
            src_ref=fin.at[peer],
            dst_ref=got.at[me],
            send_sem=asend.at[peer],
            recv_sem=arecv.at[me],
            device_id={"ctx": peer},
            device_id_type=MESH,
        )

    def state_arrival(peer):
        return pltpu.make_async_remote_copy(
            src_ref=fin.at[peer],
            dst_ref=got.at[peer],
            send_sem=asend.at[peer],
            recv_sem=arecv.at[peer],
            device_id={"ctx": peer},
            device_id_type=MESH,
        )

    def carry_copy(peer):
        return pltpu.make_async_remote_copy(
            src_ref=carry.at[peer],
            dst_ref=back.at[me],
            send_sem=bsend.at[peer],
            recv_sem=brecv.at[me],
            device_id={"ctx": peer},
            device_id_type=MESH,
        )

    def carry_arrival(peer):
        return pltpu.make_async_remote_copy(
            src_ref=carry.at[peer],
            dst_ref=back.at[peer],
            send_sem=bsend.at[peer],
            recv_sem=brecv.at[peer],
            device_id={"ctx": peer},
            device_id_type=MESH,
        )

    def each_peer(act):
        def step(i, _):
            act(lax.rem(me + i, n_ctx))
            return _

        lax.fori_loop(1, n_ctx, step, 0)

    each_peer(lambda peer: state_copy(peer).start())
    got[me] = fin[me]

    def inner_part(t, _):
        load_copy(Q2, t).wait()
        halo_copy(Q2, t).wait_recv()

        @pl.when(me == 0)
        def clear():
            hthin[2, aligned(t, LANES), :] = jnp.zeros((LANES, LANES), BF16)

        def inner_group(i):
            g = t * per_tile + i
            rows = aligned(g, GROUP)
            within[g] = jnp.dot(ptwo[g], wlong[g], preferred_element_type=F32)
            query = short_filter(extended(Q2, rows), columns(rows, 1, 0))[:, LANES:]
            qnext[g] = to_rows(query, 0, blocks, BLOCK, BLOCK)

        grouped(0, per_tile, 2, inner_group)
        return _

    half = (tiles + 1) // 2
    lax.fori_loop(0, half, inner_part, 0)
    each_peer(lambda peer: state_arrival(peer).wait_recv())

    def chain(d, value):
        carry[d] = value
        return value * decay[me] + got[d]

    lax.fori_loop(0, n_ctx, chain, jnp.zeros((share, LANES), F32))
    each_peer(lambda peer: carry_copy(peer).start())
    back[me] = carry[me]
    lax.fori_loop(half, tiles, inner_part, 0)
    each_peer(lambda peer: carry_arrival(peer).wait_recv())

    sums[...] = jnp.zeros_like(sums)

    def finish_tile(t, _):
        incoming = jnp.concatenate([back[t * cuts + c] for c in range(cuts)], axis=0)
        turned = [incoming] + [pltpu.roll(incoming, k * GROUP, 1) for k in range(1, blocks)]
        block_at = lax.shift_right_logical(lane_ids(MODES, LANES), 4)
        for i in range(per_tile):
            g = t * per_tile + i
            seed = turned[-i % blocks]
            for b in range(1, blocks):
                seed = jnp.where(block_at == b, turned[(b - i) % blocks], seed)
            high, low = split_pair(state[g] + seed * fade[g])
            carried_in[i] = jnp.concatenate([high, high, low], axis=0).T

        def finish_group(i):
            g = t * per_tile + i
            carried = jnp.dot(carried_in[i], readout[g], preferred_element_type=F32)
            long_two = (within[g] + carried).astype(BF16).astype(F32)
            gated = qnext[g] * long_two
            within[g] = gated
            square = gated * gated
            for b in range(blocks):
                low_rows = square[b * GROUP : b * GROUP + 8, :]
                sums[b] = sums[b] + (low_rows + square[b * GROUP + 8 : (b + 1) * GROUP, :])

        grouped(0, per_tile, 2, finish_group)
        return _

    lax.fori_loop(0, tiles, finish_tile, 0)

    sums_in[my_mp] = jnp.sum(sums[...], axis=1)

    def sum_copy(peer, place):
        return pltpu.make_async_remote_copy(
            src_ref=sums_in.at[my_mp],
            dst_ref=sums_in.at[place],
            send_sem=msend.at[peer],
            recv_sem=mrecv.at[place],
            device_id={"mp": peer},
            device_id_type=MESH,
        )

    mp_peers = [lax.rem(my_mp + i, n_mp) for i in range(1, n_mp)]
    for peer in mp_peers:
        sum_copy(peer, my_mp).start()
    for peer in mp_peers:
        sum_copy(peer, peer).wait_recv()
    whole = sums_in[0]
    for i in range(1, n_mp):
        whole = whole + sums_in[i]
    scale = lax.rsqrt(whole / float(n_mp * chans) + 1e-05)
    sums[...] = jnp.broadcast_to(scale[:, None, :], sums.shape)

    def out_copy(t):
        rows = aligned(t, LANES)
        return pltpu.make_async_copy(xin.at[Q1, rows, :], out.at[rows, :], osem.at[t])

    def scale_tile(t, _):
        def group_step(i, _):
            g = t * per_tile + i
            rows = aligned(g, GROUP)
            gain_c = wcol[rows, 18:19]
            gated = within[g]
            for b in range(blocks):
                scale_b = jnp.concatenate([sums[b], sums[b]], axis=0)
                piece = gated[b * GROUP : (b + 1) * GROUP, :] * scale_b * gain_c
                xin[Q1, rows, b * BLOCK : (b + 1) * BLOCK] = piece.astype(BF16)
            return _

        lax.fori_loop(0, per_tile, group_step, 0)
        out_copy(t).start()
        return _

    lax.fori_loop(0, tiles, scale_tile, 0)

    for peer in mp_peers:
        sum_copy(peer, my_mp).wait_send()
    each_peer(lambda peer: state_copy(peer).wait_send())
    each_peer(lambda peer: carry_copy(peer).wait_send())

    def drain(t, _):
        for s in range(5):
            halo_copy(s, t).wait_send()
        out_copy(t).wait()
        return _

    lax.fori_loop(0, tiles, drain, 0)


def per_device(n_ctx, n_mp, query_one, key_one, value_one, query_two, key_two, conv_weights,
               mr_filter, li_rate, li_residue, norm_gain):
    chans, length = query_one.shape
    groups = chans // GROUP
    tiles = chans // LANES
    blocks = length // BLOCK
    share = tiles * MODES // n_ctx
    any_spec = pl.BlockSpec(memory_space=pl.ANY)
    vmem_spec = pl.BlockSpec(memory_space=pltpu.VMEM)
    dma = pltpu.SemaphoreType.DMA
    message = pltpu.VMEM((n_ctx, share, LANES), F32)
    return pl.pallas_call(
        functools.partial(kernel, n_ctx, n_mp),
        out_shape=jax.ShapeDtypeStruct((chans, length), BF16),
        in_specs=[any_spec] * 5 + [vmem_spec] * 5,
        out_specs=any_spec,
        scratch_shapes=[
            pltpu.VMEM((5, chans, length), BF16),
            pltpu.VMEM((2, chans, 2 * LANES), BF16),
            pltpu.VMEM((3, chans, LANES), BF16),
            pltpu.VMEM((groups, 2 * TAPS, TAPS), BF16),
            pltpu.VMEM((groups, BLOCK, BLOCK), BF16),
            pltpu.VMEM((groups, 3 * MODES, BLOCK), BF16),
            pltpu.VMEM((groups, MODES, BLOCK), BF16),
            pltpu.VMEM((groups, GROUP * blocks, BLOCK), BF16),
            pltpu.VMEM((groups, GROUP * blocks, BLOCK), F32),
            pltpu.VMEM((groups, GROUP * blocks, BLOCK), F32),
            pltpu.VMEM((groups, MODES, LANES), F32),
            pltpu.VMEM((chans, LANES), F32),
            pltpu.VMEM((LANES, chans), F32),
            pltpu.VMEM((groups, TAPS), F32),
            pltpu.VMEM((MODES, LANES), F32),
            pltpu.VMEM((MODES, LANES), F32),
            pltpu.VMEM((groups, MODES, LANES), F32),
            pltpu.VMEM((LANES // GROUP, GROUP, length + 2 * LANES), BF16),
            pltpu.VMEM((LANES // GROUP, GROUP, length + LANES), BF16),
            pltpu.VMEM((LANES // GROUP, GROUP * blocks, 3 * MODES), BF16),
            message,
            message,
            message,
            message,
            message,
            pltpu.VMEM((blocks, 8, BLOCK), F32),
            pltpu.VMEM((n_mp, blocks, BLOCK), F32),
            dma((5, tiles)),
            dma((5, tiles)),
            dma((5, tiles)),
            dma((n_ctx,)),
            dma((n_ctx,)),
            dma((n_ctx,)),
            dma((n_ctx,)),
            dma((n_mp,)),
            dma((n_mp,)),
            dma((tiles,)),
        ],
        compiler_params=pltpu.CompilerParams(
            collective_id=0, has_side_effects=True, vmem_limit_bytes=67043328
        ),
        name="hyena_pair",
    )(
        query_one, key_one, value_one, key_two, query_two,
        jnp.transpose(conv_weights, (1, 2, 0, 3)), mr_filter, li_rate.T, li_residue.T,
        norm_gain.reshape(1, chans),
    )


def solution(mesh):
    in_specs = (
        P("mp", "ctx"),
        P("mp", "ctx"),
        P("mp", "ctx"),
        P("mp", "ctx"),
        P("mp", "ctx"),
        P(None, None, None, "mp"),
        P("mp", None),
        P("mp", None),
        P("mp", None),
        P("mp"),
    )
    return jax.shard_map(
        functools.partial(per_device, mesh.shape["ctx"], mesh.shape["mp"]),
        mesh=mesh,
        in_specs=in_specs,
        out_specs=P("mp", "ctx"),
        check_vma=False,
    )
```

```python
import functools

import jax
import jax.numpy as jnp
from jax import lax
from jax.experimental import pallas as pl
from jax.experimental.pallas import tpu as pltpu
from jax.sharding import PartitionSpec as P

GROUP = 16
TAPS = 128
BLOCK = 256
MODES = 16
LANES = 128
MESH = pl.DeviceIdType.MESH
FIRST_LIMIT = 54 * 2**20
SECOND_LIMIT = 16 * 2**20
F32 = jnp.float32
BF16 = jnp.bfloat16
Q1, K1, V1, K2, Q2 = range(5)


def aligned(index, size):
    return pl.ds(pl.multiple_of(index * size, size), size)


def lane_ids(rows, cols):
    return lax.broadcasted_iota(jnp.int32, (rows, cols), 1)


def split_pair(x):
    high = x.astype(BF16)
    low = (x - high.astype(F32)).astype(BF16)
    return high, low


def short_filter(x, taps):
    w0, w1, w2 = taps
    back_one = pltpu.roll(x, 1, 1).astype(F32)
    back_two = pltpu.roll(x, 2, 1).astype(F32)
    return w0 * x.astype(F32) + w1 * back_one + w2 * back_two


def grouped(start, stop, size, act):
    def step(j, _):
        for i in range(size):
            act(start + j * size + i)
        return _

    lax.fori_loop(0, (stop - start) // size, step, 0)


def to_rows(x, first, count, step, width):
    return jnp.concatenate(
        [x[:, first + i * step : first + i * step + width] for i in range(count)], axis=0
    )


def kernel(
    n_ctx, n_mp, q1, k1, v1, k2, q2, cw, mr, rate, residue, gain,
    within, scale_out, xin, hwide, hthin, wmed, wlong, readout, proj, ptwo, qnext, state, wcol,
    pad, tapf, rate_t, res_t, fade, prod, mid, carried_in, fin, decay, got, carry, back, sums, sums_in,
    in_sem, hsend, hrecv, asend, arecv, bsend, brecv, msend, mrecv,
):
    me = lax.axis_index("ctx")
    my_mp = lax.axis_index("mp")
    right = lax.rem(me + 1, n_ctx)
    chans, length = xin.shape[1:]
    tiles = chans // LANES
    per_tile = LANES // GROUP
    groups = chans // GROUP
    blocks = length // BLOCK
    med_blocks = length // TAPS
    share = tiles * MODES // n_ctx
    cuts = MODES // share
    streams = (q1, k1, v1, k2, q2)

    def load_copy(s, t):
        rows = aligned(t, LANES)
        return pltpu.make_async_copy(streams[s].at[rows, :], xin.at[s, rows, :], in_sem.at[s, t])

    def halo_copy(s, t):
        rows = aligned(t, LANES)
        wide = s in (K1, V1)
        width = 2 * LANES if wide else LANES
        target = hwide.at[s - K1, rows, :] if wide else hthin.at[{Q1: 0, K2: 1, Q2: 2}[s], rows, :]
        return pltpu.make_async_remote_copy(
            src_ref=streams[s].at[rows, pl.ds(length - width, width)],
            dst_ref=target,
            send_sem=hsend.at[s, t],
            recv_sem=hrecv.at[s, t],
            device_id={"ctx": right},
            device_id_type=MESH,
        )

    first_four = (K1, V1, Q1, K2)

    def start_loads(t, _):
        for s in first_four:
            load_copy(s, t).start()
        return _

    lax.fori_loop(0, tiles, start_loads, 0)

    def start_late(t, _):
        load_copy(Q2, t).start()
        return _

    lax.fori_loop(0, tiles, start_late, 0)

    barrier = pltpu.get_barrier_semaphore()

    def greet_ctx(i, _):
        pl.semaphore_signal(
            barrier, inc=1, device_id={"ctx": lax.rem(me + i, n_ctx)}, device_id_type=MESH
        )
        return _

    lax.fori_loop(1, n_ctx, greet_ctx, 0)
    for i in range(1, n_mp):
        pl.semaphore_signal(
            barrier, inc=1, device_id={"mp": lax.rem(my_mp + i, n_mp)}, device_id_type=MESH
        )

    pad[...] = jnp.zeros_like(pad)
    for layer in range(2):
        for stream in range(3):
            for tap in range(3):
                at = layer * 9 + stream * 3 + tap
                pad[at : at + 1, :] = cw[stream, tap, layer : layer + 1, :]
    pad[18:19, :] = gain[...]
    for t in range(tiles):
        wcol[t * LANES : (t + 1) * LANES, :] = pad[:, t * LANES : (t + 1) * LANES].T
    tapf[...] = mr[...].astype(F32)
    rate_t[...] = jnp.zeros_like(rate_t)
    res_t[...] = jnp.zeros_like(res_t)
    rate_t[:, 0:groups] = rate[...]
    res_t[:, 0:groups] = residue[...]

    def mode_column(table, g):
        hit = lane_ids(MODES, LANES) == g
        return jnp.sum(jnp.where(hit, table[...], 0.0), axis=1, keepdims=True)

    def circulant(row):
        return pltpu.roll(
            jnp.broadcast_to(row, (LANES, LANES)), 0, 1, stride=1, stride_axis=0
        )

    def tables(g):
        above = lane_ids(LANES, LANES) >= lax.broadcasted_iota(jnp.int32, (LANES, LANES), 0)
        rate_c = mode_column(rate_t, g)
        amp = mode_column(res_t, g) * jnp.sqrt(rate_c)
        lag = lane_ids(1, BLOCK).astype(F32)
        fall = jnp.exp(-rate_c * lag)
        proj[g] = jnp.exp(-rate_c * (float(BLOCK - 1) - lag)).astype(BF16)
        tall = amp * fall
        high, low = split_pair(tall * jnp.exp(-rate_c))
        readout[g] = jnp.concatenate([high, low, high], axis=0)
        taps_h = jnp.sum(tall, axis=0, keepdims=True)
        near = circulant(taps_h[:, :LANES])
        far = circulant(taps_h[:, LANES:])
        diagonal = jnp.where(above, near, 0.0).astype(BF16)
        wlong[g, 0:LANES, 0:LANES] = diagonal
        wlong[g, LANES:, LANES:] = diagonal
        wlong[g, 0:LANES, LANES:] = jnp.where(above, far, near).astype(BF16)
        wlong[g, LANES:, 0:LANES] = jnp.zeros((LANES, LANES), BF16)
        short = circulant(tapf[pl.ds(g, 1), :])
        wmed[g, 0:LANES, :] = jnp.where(above, 0.0, short).astype(BF16)
        wmed[g, LANES:, :] = jnp.where(above, short, 0.0).astype(BF16)
        block_at = lax.shift_right_logical(lane_ids(MODES, LANES), 4).astype(F32)
        fade[g] = jnp.exp(-rate_c * (block_at * float(BLOCK)))

    early = groups // 2
    grouped(0, early, 2, tables)
    pl.semaphore_wait(barrier, n_ctx - 1 + n_mp - 1)

    def start_halos(t, _):
        for s in first_four:
            halo_copy(s, t).start()
        return _

    lax.fori_loop(0, tiles, start_halos, 0)

    def start_late_halos(t, _):
        halo_copy(Q2, t).start()
        return _

    lax.fori_loop(0, tiles, start_late_halos, 0)
    grouped(early, groups, 2, tables)

    def columns(rows, layer, stream):
        at = layer * 9 + stream * 3
        return [wcol[rows, at + tap : at + tap + 1] for tap in range(3)]

    def extended(s, rows):
        wide = s in (K1, V1)
        halo = hwide[s - K1, rows, :] if wide else hthin[{Q1: 0, K2: 1, Q2: 2}[s], rows, :]
        return jnp.concatenate([halo, xin[s, rows, :]], axis=1)

    def make_product(t, i):
        rows = aligned(t * per_tile + i, GROUP)
        key = short_filter(extended(K1, rows), columns(rows, 0, 1))
        value = short_filter(extended(V1, rows), columns(rows, 0, 2))
        prod[i] = (key * value).astype(BF16)

    def make_layer(t, i):
        g = t * per_tile + i
        rows = aligned(g, GROUP)
        mixed = jnp.dot(
            to_rows(prod[i], 0, med_blocks + 1, TAPS, 2 * TAPS), wmed[g], preferred_element_type=F32
        )
        mixed = jnp.concatenate(
            [mixed[j * GROUP : (j + 1) * GROUP, :] for j in range(med_blocks + 1)], axis=1
        )
        query = short_filter(extended(Q1, rows), columns(rows, 0, 0))
        mid[i] = (query * mixed).astype(BF16)

    def make_second(t, i):
        g = t * per_tile + i
        rows = aligned(g, GROUP)
        value_two = short_filter(mid[i], columns(rows, 1, 2))[:, LANES:]
        key_two = short_filter(extended(K2, rows), columns(rows, 1, 1))[:, LANES:]
        second = (key_two * value_two).astype(BF16)
        ptwo[g] = to_rows(second, 0, blocks, BLOCK, BLOCK)

    def make_states(t):
        lane = lane_ids(MODES, GROUP * blocks)
        ends = jnp.zeros((MODES, LANES), F32)
        drops = jnp.zeros((MODES, LANES), F32)
        for i in range(per_tile):
            g = t * per_tile + i
            total = lax.dot_general(
                proj[g], ptwo[g], (((1,), (1,)), ((), ())), preferred_element_type=F32
            )
            rate_c = mode_column(rate_t, g)
            width = 1
            while width < blocks:
                moved = pltpu.roll(total, width * GROUP, 1)
                factor = jnp.exp(-rate_c * float(BLOCK * width))
                total = total + jnp.where(lane >= width * GROUP, factor * moved, 0.0)
                width *= 2
            state[g] = jnp.where(lane >= GROUP, pltpu.roll(total, GROUP, 1), 0.0)
            spot = lax.shift_right_logical(lane, 4) == i
            moved = pltpu.roll(total, (i + 1) * GROUP % LANES, 1) if i + 1 < blocks else total
            ends = jnp.where(spot, moved, ends)
            drops = jnp.where(spot, jnp.exp(-rate_c * float(length)), drops)
        for c in range(cuts):
            part = slice(c * share, (c + 1) * share)
            fin[t * cuts + c] = ends[part]
            decay[t * cuts + c] = drops[part]

    def tile_step(t, _):
        for s in first_four:
            load_copy(s, t).wait()
            halo_copy(s, t).wait_recv()

        @pl.when(me == 0)
        def clear():
            rows = aligned(t, LANES)
            hwide[:, rows, :] = jnp.zeros((2, LANES, 2 * LANES), BF16)
            hthin[0:2, rows, :] = jnp.zeros((2, LANES, LANES), BF16)

        grouped(0, per_tile, 4, functools.partial(make_product, t))
        grouped(0, per_tile, 4, functools.partial(make_layer, t))
        grouped(0, per_tile, 4, functools.partial(make_second, t))
        make_states(t)
        return _

    lax.fori_loop(0, tiles, tile_step, 0)

    def state_copy(peer):
        return pltpu.make_async_remote_copy(
            src_ref=fin.at[peer],
            dst_ref=got.at[me],
            send_sem=asend.at[peer],
            recv_sem=arecv.at[me],
            device_id={"ctx": peer},
            device_id_type=MESH,
        )

    def state_arrival(peer):
        return pltpu.make_async_remote_copy(
            src_ref=fin.at[peer],
            dst_ref=got.at[peer],
            send_sem=asend.at[peer],
            recv_sem=arecv.at[peer],
            device_id={"ctx": peer},
            device_id_type=MESH,
        )

    def carry_copy(peer):
        return pltpu.make_async_remote_copy(
            src_ref=carry.at[peer],
            dst_ref=back.at[me],
            send_sem=bsend.at[peer],
            recv_sem=brecv.at[me],
            device_id={"ctx": peer},
            device_id_type=MESH,
        )

    def carry_arrival(peer):
        return pltpu.make_async_remote_copy(
            src_ref=carry.at[peer],
            dst_ref=back.at[peer],
            send_sem=bsend.at[peer],
            recv_sem=brecv.at[peer],
            device_id={"ctx": peer},
            device_id_type=MESH,
        )

    def each_peer(act):
        def step(i, _):
            act(lax.rem(me + i, n_ctx))
            return _

        lax.fori_loop(1, n_ctx, step, 0)

    each_peer(lambda peer: state_copy(peer).start())
    got[me] = fin[me]

    def inner_part(t, _):
        load_copy(Q2, t).wait()
        halo_copy(Q2, t).wait_recv()

        @pl.when(me == 0)
        def clear():
            hthin[2, aligned(t, LANES), :] = jnp.zeros((LANES, LANES), BF16)

        def inner_group(i):
            g = t * per_tile + i
            rows = aligned(g, GROUP)
            within[g] = jnp.dot(ptwo[g], wlong[g], preferred_element_type=F32)
            query = short_filter(extended(Q2, rows), columns(rows, 1, 0))[:, LANES:]
            qnext[g] = to_rows(query, 0, blocks, BLOCK, BLOCK)

        grouped(0, per_tile, 4, inner_group)
        return _

    half = (tiles + 1) // 2
    lax.fori_loop(0, half, inner_part, 0)
    each_peer(lambda peer: state_arrival(peer).wait_recv())

    def chain(d, value):
        carry[d] = value
        return value * decay[me] + got[d]

    lax.fori_loop(0, n_ctx, chain, jnp.zeros((share, LANES), F32))
    each_peer(lambda peer: carry_copy(peer).start())
    back[me] = carry[me]
    lax.fori_loop(half, tiles, inner_part, 0)
    each_peer(lambda peer: carry_arrival(peer).wait_recv())

    sums[...] = jnp.zeros_like(sums)

    def finish_tile(t, _):
        incoming = jnp.concatenate([back[t * cuts + c] for c in range(cuts)], axis=0)
        turned = [incoming] + [pltpu.roll(incoming, k * GROUP, 1) for k in range(1, blocks)]
        block_at = lax.shift_right_logical(lane_ids(MODES, LANES), 4)
        for i in range(per_tile):
            g = t * per_tile + i
            seed = turned[-i % blocks]
            for b in range(1, blocks):
                seed = jnp.where(block_at == b, turned[(b - i) % blocks], seed)
            high, low = split_pair(state[g] + seed * fade[g])
            carried_in[i] = jnp.concatenate([high, high, low], axis=0).T

        def gain_rows(g):
            gain_c = wcol[aligned(g, GROUP), 18:19]
            return jnp.concatenate([gain_c] * blocks, axis=0)

        def finish_group(i):
            g = t * per_tile + i
            carried = jnp.dot(carried_in[i], readout[g], preferred_element_type=F32)
            long_two = (within[g] + carried).astype(BF16).astype(F32)
            gated = qnext[g] * long_two
            within[g] = gated * gain_rows(g)
            square = gated * gated
            for b in range(blocks):
                low_rows = square[b * GROUP : b * GROUP + 8, :]
                sums[b] = sums[b] + (low_rows + square[b * GROUP + 8 : (b + 1) * GROUP, :])

        grouped(0, per_tile, 4, finish_group)
        return _

    lax.fori_loop(0, tiles, finish_tile, 0)

    sums_in[my_mp] = jnp.sum(sums[...], axis=1)

    def sum_copy(peer, place):
        return pltpu.make_async_remote_copy(
            src_ref=sums_in.at[my_mp],
            dst_ref=sums_in.at[place],
            send_sem=msend.at[peer],
            recv_sem=mrecv.at[place],
            device_id={"mp": peer},
            device_id_type=MESH,
        )

    mp_peers = [lax.rem(my_mp + i, n_mp) for i in range(1, n_mp)]
    for peer in mp_peers:
        sum_copy(peer, my_mp).start()
    for peer in mp_peers:
        sum_copy(peer, peer).wait_recv()
    whole = sums_in[0]
    for i in range(1, n_mp):
        whole = whole + sums_in[i]
    scale_out[...] = lax.rsqrt(whole / float(n_mp * chans) + 1e-05)

    for peer in mp_peers:
        sum_copy(peer, my_mp).wait_send()
    each_peer(lambda peer: state_copy(peer).wait_send())
    each_peer(lambda peer: carry_copy(peer).wait_send())

    def drain(t, _):
        for s in range(5):
            halo_copy(s, t).wait_send()
        return _

    lax.fori_loop(0, tiles, drain, 0)


def scale_kernel(weighted, scale, out, made, osem):
    groups, _, block = weighted.shape
    blocks = scale.shape[0]
    per_tile = LANES // GROUP

    def out_copy(t):
        rows = aligned(t, LANES)
        return pltpu.make_async_copy(made.at[rows, :], out.at[rows, :], osem.at[t])

    tiles = groups // per_tile

    def scale_tile(t, carry):
        def scale_group(i):
            g = t * per_tile + i
            rows = aligned(g, GROUP)
            for b in range(blocks):
                piece = weighted[g, b * GROUP : (b + 1) * GROUP, :] * scale[b : b + 1, :]
                made[rows, b * block : (b + 1) * block] = piece.astype(BF16)

        grouped(0, per_tile, 4, scale_group)
        out_copy(t).start()
        return carry

    lax.fori_loop(0, tiles, scale_tile, 0)

    def drain(t, carry):
        out_copy(t).wait()
        return carry

    lax.fori_loop(0, tiles, drain, 0)


def per_device(n_ctx, n_mp, query_one, key_one, value_one, query_two, key_two, conv_weights,
               mr_filter, li_rate, li_residue, norm_gain):
    chans, length = query_one.shape
    groups = chans // GROUP
    tiles = chans // LANES
    blocks = length // BLOCK
    share = tiles * MODES // n_ctx
    any_spec = pl.BlockSpec(memory_space=pl.ANY)
    vmem_spec = pl.BlockSpec(memory_space=pltpu.VMEM)
    dma = pltpu.SemaphoreType.DMA
    message = pltpu.VMEM((n_ctx, share, LANES), F32)
    weighted, scale = pl.pallas_call(
        functools.partial(kernel, n_ctx, n_mp),
        out_shape=(pltpu.VMEM((groups, GROUP * blocks, BLOCK), F32), pltpu.VMEM((blocks, BLOCK), F32)),
        in_specs=[any_spec] * 5 + [vmem_spec] * 5,
        out_specs=(vmem_spec, vmem_spec),
        scratch_shapes=[
            pltpu.VMEM((5, chans, length), BF16),
            pltpu.VMEM((2, chans, 2 * LANES), BF16),
            pltpu.VMEM((3, chans, LANES), BF16),
            pltpu.VMEM((groups, 2 * TAPS, TAPS), BF16),
            pltpu.VMEM((groups, BLOCK, BLOCK), BF16),
            pltpu.VMEM((groups, 3 * MODES, BLOCK), BF16),
            pltpu.VMEM((groups, MODES, BLOCK), BF16),
            pltpu.VMEM((groups, GROUP * blocks, BLOCK), BF16),
            pltpu.VMEM((groups, GROUP * blocks, BLOCK), F32),
            pltpu.VMEM((groups, MODES, LANES), F32),
            pltpu.VMEM((chans, LANES), F32),
            pltpu.VMEM((LANES, chans), F32),
            pltpu.VMEM((groups, TAPS), F32),
            pltpu.VMEM((MODES, LANES), F32),
            pltpu.VMEM((MODES, LANES), F32),
            pltpu.VMEM((groups, MODES, LANES), F32),
            pltpu.VMEM((LANES // GROUP, GROUP, length + 2 * LANES), BF16),
            pltpu.VMEM((LANES // GROUP, GROUP, length + LANES), BF16),
            pltpu.VMEM((LANES // GROUP, GROUP * blocks, 3 * MODES), BF16),
            message,
            message,
            message,
            message,
            message,
            pltpu.VMEM((blocks, 8, BLOCK), F32),
            pltpu.VMEM((n_mp, blocks, BLOCK), F32),
            dma((5, tiles)),
            dma((5, tiles)),
            dma((5, tiles)),
            dma((n_ctx,)),
            dma((n_ctx,)),
            dma((n_ctx,)),
            dma((n_ctx,)),
            dma((n_mp,)),
            dma((n_mp,)),
        ],
        compiler_params=pltpu.CompilerParams(
            collective_id=0, has_side_effects=True, vmem_limit_bytes=FIRST_LIMIT
        ),
        name="hyena_pair",
    )(
        query_one, key_one, value_one, key_two, query_two,
        jnp.transpose(conv_weights, (1, 2, 0, 3)), mr_filter, li_rate.T, li_residue.T,
        norm_gain.reshape(1, chans),
    )
    return pl.pallas_call(
        scale_kernel,
        out_shape=jax.ShapeDtypeStruct((chans, length), BF16),
        in_specs=[vmem_spec, vmem_spec],
        out_specs=any_spec,
        scratch_shapes=[pltpu.VMEM((chans, length), BF16), dma((tiles,))],
        compiler_params=pltpu.CompilerParams(vmem_limit_bytes=SECOND_LIMIT),
        name="scale_rows",
    )(weighted, scale)


def solution(mesh):
    in_specs = (
        P("mp", "ctx"),
        P("mp", "ctx"),
        P("mp", "ctx"),
        P("mp", "ctx"),
        P("mp", "ctx"),
        P(None, None, None, "mp"),
        P("mp", None),
        P("mp", None),
        P("mp", None),
        P("mp"),
    )
    return jax.shard_map(
        functools.partial(per_device, mesh.shape["ctx"], mesh.shape["mp"]),
        mesh=mesh,
        in_specs=in_specs,
        out_specs=P("mp", "ctx"),
        check_vma=False,
    )
```
